256 devices in a mesh: seq: 32 (over z_lo, y, core), batch: 8 (over x, z_hi).
Axes of the slice: x: 4, y: 4, z: 8 (z_hi: 2, z_lo: 4; z = z_hi * 4 + z_lo), core: 2. Of those that a mesh axis runs over, the one named last changes fastest.
Arguments:
- coarse: bfloat16 [8, 8192, 1536], P('batch', 'seq'), may hold values from -6 to 6
- skip: bfloat16 [8, 16384, 1536], P('batch', 'seq'), may hold values from -6 to 6
- depth_kernel: float32 [3, 1536], replicated, may hold values from -3.5 to 3.5
- sep_weight: bfloat16 [1536, 1536], P('seq'), may hold values from -0.15625 to 0.15625
- sep_bias: float32 [1536], replicated, may hold values from -3 to 3
- head_weight: bfloat16 [1536, 3840], P(None, 'seq'), may hold values from -0.15625 to 0.15625
- head_bias: float32 [3840], replicated, may hold values from -4 to 4
- strand_pair: int32 [3840], replicated, may hold values from 0 to 3839, as said below
Outputs:
- preds: bfloat16 [8, 16384, 3840], P('batch', 'seq')
The draws below stay inside these ranges and needn't reach their ends.
Inputs may be any that keep to these rules, and one draw needn't show every extreme that they name: strand_pair is a permutation with strand_pair[strand_pair[t]] == t; about half of the tracks are paired with another one.
All inputs are finite; a program needn't handle non-finite values.
Results may differ from the reference program's by a relative error of at most 0.0053.
Values may be sent and summed in bfloat16 or wider, within the bound.
A program may use at most 64 MiB of HBM per device.

```python
import jax
import jax.numpy as jnp
from jax import lax

D = 1536
TRACKS = 3840
NB = 16384
NC = 8192
SEQS = 4
ROWS = 8


def draw_strand_pair(key, part):
    order = jax.random.permutation(key, TRACKS).astype(jnp.int32)
    paired = TRACKS // 4
    first_half = order[:paired]
    second_half = order[paired:2 * paired]
    table = jnp.arange(TRACKS, dtype=jnp.int32)
    table = table.at[first_half].set(second_half).at[second_half].set(first_half)
    return table.astype(jnp.int32)


def steps_of(key, shape, cuts, least, high):
    def one(dim, parts):
        draws = jax.random.uniform(jax.random.fold_in(jax.random.fold_in(key, 6), dim), (parts,), jnp.float32, least / len(cuts), high / len(cuts))
        return jnp.repeat(jnp.exp(draws), shape[dim] // parts).reshape((-1,) + (1,) * (len(shape) - dim - 1))

    gain = one(*cuts[0])
    for cut in cuts[1:]:
        gain = gain * one(*cut)
    return gain


def gaussian(key, dims, spread, limit, split=(), kind=jnp.bfloat16):
    loudness = steps_of(key, dims, split, -0.22, 0.18) if split else 1.0
    result = jax.random.normal(key, dims, jnp.float32) * spread * loudness
    return jnp.minimum(jnp.maximum(result, -limit), limit).astype(kind)


def setup_inputs(seed: int = 0) -> dict:
    key_of = jax.random.split(jax.random.key(seed), 9)
    coarse = gaussian(key_of[0], (ROWS, NC, D), 1.0, 6.0, ((0, 8), (1, 32)))
    skip = gaussian(key_of[1], (ROWS, NB, D), 1.0, 6.0, ((0, 8), (1, 32)))
    depth_kernel = gaussian(key_of[2], (3, D), 3 ** -0.5, 3.5, (), jnp.float32)
    sep_weight = gaussian(key_of[3], (D, D), D ** -0.5, 0.15625, ((0, 32),))
    sep_bias = gaussian(key_of[4], (D,), 0.5, 3.0, (), jnp.float32)
    head_weight = gaussian(key_of[5], (D, TRACKS), D ** -0.5, 0.15625, ((1, 32),))
    head_bias = gaussian(key_of[6], (TRACKS,), 1.0, 4.0, (), jnp.float32)
    strand_pair = draw_strand_pair(jax.random.fold_in(key_of[8], 71), 0)
    return dict(coarse=coarse, skip=skip, depth_kernel=depth_kernel, sep_weight=sep_weight, sep_bias=sep_bias, head_weight=head_weight, head_bias=head_bias, strand_pair=strand_pair)


def strand_head(inputs, depth_kernel, sep_weight, sep_bias, head_weight, head_bias):
    coarse_row, skip_row = inputs
    upsampled = jnp.repeat(coarse_row.astype(jnp.float32), 2, axis=0)
    merged = (upsampled + skip_row.astype(jnp.float32)).astype(jnp.bfloat16)
    padded = jnp.pad(merged, ((1, 1), (0, 0)))
    depthwise = depth_kernel[0] * padded[:-2] + depth_kernel[1] * padded[1:-1] + depth_kernel[2] * padded[2:]
    depthwise = depthwise.astype(jnp.bfloat16)
    pointwise = jnp.dot(depthwise, sep_weight, preferred_element_type=jnp.float32) + sep_bias
    features = jax.nn.gelu(pointwise, approximate=True).astype(jnp.bfloat16)
    logits = jnp.dot(features, head_weight, preferred_element_type=jnp.float32) + head_bias
    return jax.nn.softplus(logits).astype(jnp.bfloat16)


def reference(coarse, skip, depth_kernel, sep_weight, sep_bias, head_weight, head_bias, strand_pair):
    strand_heads = lax.map(lambda inputs: strand_head(inputs, depth_kernel, sep_weight, sep_bias, head_weight, head_bias), (coarse, skip))
    partner = jnp.concatenate([strand_heads[SEQS:], strand_heads[:SEQS]], axis=0)
    partner = jnp.take(partner[:, ::-1], strand_pair, axis=2)
    averaged = 0.5 * (strand_heads.astype(jnp.float32) + partner.astype(jnp.float32))
    return averaged.astype(jnp.bfloat16)
```

```python
import jax
import jax.numpy as jnp
from jax import lax
from jax.sharding import PartitionSpec as P


def with_halo(cells, axis, width):
    count = lax.axis_size(axis)
    ends = count - 1
    head = lax.slice_in_dim(cells, 0, width, axis=0)
    tail = lax.slice_in_dim(cells, cells.shape[0] - width, cells.shape[0], axis=0)
    return jnp.concatenate(
        [
            lax.ppermute(tail, axis, [(i, (i + 1) % count) for i in range(ends)]),
            cells,
            lax.ppermute(head, axis, [((i + 1) % count, i) for i in range(ends)]),
        ],
        axis=0,
    )


def reversed_rows(x):
    rows = x.shape[0]
    r = lax.broadcasted_iota(jnp.int32, (rows, rows), 0)
    c = lax.broadcasted_iota(jnp.int32, (rows, rows), 1)
    flip = (r + c == rows - 1).astype(x.dtype)
    return jnp.dot(flip, x, preferred_element_type=jnp.float32).astype(x.dtype)


def to_mirror(x):
    nb, ns = lax.axis_size("batch"), lax.axis_size("seq")
    half = nb // 2
    route = []
    for s in range(ns):
        for b in range(nb):
            mirror = (ns - 1 - s) * nb + (b + half) % nb
            route.append((s * nb + b, mirror))
    return lax.ppermute(x, ("seq", "batch"), route)


def per_device(
    coarse, skip, depth_kernel, sep_weight, sep_bias, head_weight, head_bias, strand_pair
):
    sep_full = lax.all_gather(sep_weight, "seq", axis=0, tiled=True)
    head_full = lax.all_gather(head_weight, "seq", axis=1, tiled=True)
    upsampled = jnp.repeat(coarse[0].astype(jnp.float32), 2, axis=0)
    merged = (upsampled + skip[0]).astype(jnp.bfloat16)
    padded = with_halo(merged, "seq", 1)
    depthwise = (
        depth_kernel[0] * padded[:-2]
        + depth_kernel[1] * padded[1:-1]
        + depth_kernel[2] * padded[2:]
    )
    depthwise = depthwise.astype(jnp.bfloat16)
    mirrored = to_mirror(reversed_rows(depthwise))

    def head(block):
        pointwise = jnp.dot(block, sep_full, preferred_element_type=jnp.float32)
        features = jax.nn.gelu(pointwise + sep_bias, approximate=True).astype(jnp.bfloat16)
        logits = jnp.dot(features, head_full, preferred_element_type=jnp.float32)
        return jax.nn.softplus(logits + head_bias).astype(jnp.bfloat16)

    own = head(depthwise)
    other = jnp.take(head(mirrored), strand_pair, axis=1)
    averaged = 0.5 * (own.astype(jnp.float32) + other.astype(jnp.float32))
    return averaged.astype(jnp.bfloat16)[None]


def solution(mesh):
    in_specs = (
        P("batch", "seq", None),
        P("batch", "seq", None),
        P(),
        P("seq", None),
        P(),
        P(None, "seq"),
        P(),
        P(),
    )
    return jax.shard_map(
        per_device,
        mesh=mesh,
        in_specs=in_specs,
        out_specs=P("batch", "seq", None),
        check_vma=False,
    )
```

```python
import jax
import jax.numpy as jnp
from jax import lax
from jax.experimental import pallas as pl
from jax.experimental.pallas import tpu as pltpu
from jax.sharding import PartitionSpec as P

ROWS = 512
D = 1536
TRACKS = 3840
SHARD = 120
LANES = 128
BLOCKS = 16
SEP_ROWS = 48
QUARTER = 384
CHUNKS = 4
CHUNK = ROWS // CHUNKS
DYS = (1, 3, 2)


def with_halo(cells, axis, width):
    count = lax.axis_size(axis)
    ends = count - 1
    head = lax.slice_in_dim(cells, 0, width, axis=0)
    tail = lax.slice_in_dim(cells, cells.shape[0] - width, cells.shape[0], axis=0)
    return jnp.concatenate(
        [
            lax.ppermute(tail, axis, [(i, (i + 1) % count) for i in range(ends)]),
            cells,
            lax.ppermute(head, axis, [((i + 1) % count, i) for i in range(ends)]),
        ],
        axis=0,
    )


def reversed_rows(x):
    rows = x.shape[0]
    r = lax.broadcasted_iota(jnp.int32, (rows, rows), 0)
    c = lax.broadcasted_iota(jnp.int32, (rows, rows), 1)
    flip = (r + c == rows - 1).astype(x.dtype)
    return jnp.dot(flip, x, preferred_element_type=jnp.float32).astype(x.dtype)


def gelu(v):
    return 0.5 * v * (1.0 + jnp.tanh(0.7978845608028654 * (v + 0.044715 * v * v * v)))


def softplus(v):
    return jnp.maximum(v, 0.0) + jnp.log1p(jnp.exp(-jnp.abs(v)))


def kernel(
    dw, rev, sep_in, head_in, sep_b, head_b, pos,
    out,
    wsep, whead, mirrored, feat, hown, hpart, stage,
    local_sem, ex_send, ex_recv, z_send, z_recv, y_send, y_recv, x_send, x_recv,
    s_send, s_recv, out_sem,
):
    s = lax.axis_index("seq")
    b = lax.axis_index("batch")
    c = s % 2
    y = (s // 2) % 4
    zl = s // 8
    x = b // 2
    zh = b % 2
    z = zh * 4 + zl
    u = (5 - zl) % 4

    def device(zz, yy, xx, cc):
        return {"seq": ((zz % 4) * 4 + yy) * 2 + cc, "batch": xx * 2 + zz // 4}

    mirror = {"seq": 31 - s, "batch": (b + 4) % 8}
    sibling = device(z, y, x, 1 - c)
    z_dev = [None] + [device((z + u - (u + k) % 4 + 8) % 8, y, x, c) for k in (1, 2, 3)]
    y_dev = {d: device(z, (y + d) % 4, x, c) for d in (1, 2, 3)}
    x_dev = {d: device(z, y, (x + d) % 4, c) for d in (1, 2, 3)}

    barrier = pltpu.get_barrier_semaphore()
    peers = [mirror, sibling] + z_dev[1:] + list(y_dev.values()) + list(x_dev.values())
    for peer in peers:
        pl.semaphore_signal(barrier, inc=1, device_id=peer, device_id_type=pl.DeviceIdType.MESH)
    pl.semaphore_wait(barrier, len(peers))

    def slot(k, dy):
        return ((zl + k) % 4) * 4 + (y + dy) % 4

    def view(p, j, cc, q=None):
        if p == 0:
            rows = pl.ds(pl.multiple_of((j * 2 + cc) * SEP_ROWS, 16), SEP_ROWS)
            if q is None:
                return wsep.at[rows, :]
            return wsep.at[rows, pl.ds(pl.multiple_of(q * QUARTER, LANES), QUARTER)]
        lanes = pl.ds(pl.multiple_of(cc * LANES, LANES), LANES)
        if q is None:
            return whead.at[j, :, lanes]
        return whead.at[j, pl.ds(pl.multiple_of(q * QUARTER, LANES), QUARTER), lanes]

    def own_view(p, q=None):
        if p == 0:
            if q is None:
                return sep_in
            return sep_in.at[:, pl.ds(pl.multiple_of(q * QUARTER, LANES), QUARTER)]
        if q is None:
            return head_in
        return head_in.at[pl.ds(pl.multiple_of(q * QUARTER, LANES), QUARTER), :]

    def copy(src, dst, send, recv, to):
        return pltpu.make_async_remote_copy(
            src_ref=src, dst_ref=dst, send_sem=send, recv_sem=recv,
            device_id=to, device_id_type=pl.DeviceIdType.MESH,
        )

    def z_copy(p, k):
        return copy(own_view(p), view(p, slot(0, 0), c), z_send.at[p, k - 1], z_recv.at[p, k - 1], z_dev[k])

    def y_copy(p, k, d):
        i = DYS.index(d)
        q = x if d == 2 else None
        src = own_view(p, q) if k == 0 else view(p, slot(k, 0), c, q)
        return copy(src, view(p, slot(k, 0), c, q), y_send.at[p, k, i], y_recv.at[p, k, i], y_dev[d])

    def x_copy(p, k, d):
        ref = view(p, slot(k, 2), c, x)
        return copy(ref, ref, x_send.at[p, k, d - 1], x_recv.at[p, k, d - 1], x_dev[d])

    def s_copy(p, k, dy):
        src = own_view(p) if k == 0 and dy == 0 else view(p, slot(k, dy), c)
        return copy(src, view(p, slot(k, dy), c), s_send.at[p, k, dy], s_recv.at[p, k, dy], sibling)

    def arrived(dst, recv):
        copy(dst, dst, s_send.at[0, 0, 0], recv, sibling).wait_recv()

    def z_wait(p, k):
        arrived(view(p, slot(k, 0), c), z_recv.at[p, k - 1])

    def y_wait(p, k, d):
        i = DYS.index((4 - d) % 4)
        q = x if d == 2 else None
        arrived(view(p, slot(k, d), c, q), y_recv.at[p, k, i])

    def x_wait(p, k, d):
        arrived(view(p, slot(k, 2), c, (x + 4 - d) % 4), x_recv.at[p, k, d - 1])

    def s_wait(p, k, dy):
        arrived(view(p, slot(k, dy), 1 - c), s_recv.at[p, k, dy])

    def ex_copy(i):
        rows = pl.ds(i * CHUNK, CHUNK)
        return copy(rev.at[rows, :], mirrored.at[rows, :], ex_send.at[i], ex_recv.at[i], mirror)

    def spread(p, k):
        for d in (2, 1, 3):
            y_copy(p, k, d).start()
        s_copy(p, k, 0).start()

    locals_ = [
        pltpu.make_async_copy(own_view(p), view(p, slot(0, 0), c), local_sem.at[p]) for p in (0, 1)
    ]
    for cp in locals_:
        cp.start()
    for p in (0, 1):
        for k in (1, 2, 3):
            z_copy(p, k).start()
        spread(p, 0)
        if p == 0:
            for i in range(CHUNKS):
                ex_copy(i).start()

    def z_stage(p):
        for k in (1, 2, 3):
            z_wait(p, k)
            spread(p, k)

    def q_stage(p):
        for k in range(4):
            y_wait(p, k, 2)
            for d in (2, 1, 3):
                x_copy(p, k, d).start()

    def last_stage(p):
        for k in range(4):
            for d in (1, 3):
                y_wait(p, k, d)
                s_copy(p, k, d).start()
        for k in range(4):
            for d in (1, 3, 2):
                x_wait(p, k, d)
            s_copy(p, k, 2).start()

    def from_sibling(p):
        for k in range(4):
            for dy in range(4):
                s_wait(p, k, dy)

    z_stage(0)
    q_stage(0)
    z_stage(1)
    last_stage(0)
    for cp in locals_:
        cp.wait()
    from_sibling(0)

    def features(block):
        @pl.loop(0, D // 256)
        def _(n):
            cols = pl.ds(pl.multiple_of(n * 256, 256), 256)
            v = jnp.dot(block[...], wsep[:, cols], preferred_element_type=jnp.float32)
            feat[:, cols] = gelu(v + sep_b[:, cols]).astype(jnp.bfloat16)

    def head(dst):
        @pl.loop(0, BLOCKS)
        def _(j):
            cols = pl.ds(pl.multiple_of(j * 256, 256), 256)
            v = jnp.dot(feat[...], whead[j], preferred_element_type=jnp.float32)
            dst[:, cols] = softplus(v + head_b[:, cols]).astype(jnp.bfloat16)

    features(dw)
    q_stage(1)
    last_stage(1)
    from_sibling(1)
    head(hown)
    for i in range(CHUNKS):
        rows = pl.ds(i * CHUNK, CHUNK)
        arrived(mirrored.at[rows, :], ex_recv.at[i])
    features(mirrored)
    head(hpart)

    def out_copy(n, i):
        cols = pl.ds(pl.multiple_of(n * 256, 256), 256)
        return pltpu.make_async_copy(stage.at[i], out.at[:, cols], out_sem.at[i])

    row = lax.broadcasted_iota(jnp.int32, (512, 256), 0)
    col = lax.broadcasted_iota(jnp.int32, (1, 256), 1)
    tiles = TRACKS // 256

    def ones_at(place):
        return jnp.where(row == place, 1.0, 0.0).astype(jnp.bfloat16)

    @pl.loop(0, tiles)
    def _(n):
        i = n % 2
        cols = pl.ds(pl.multiple_of(n * 256, 256), 256)
        track = n * 256 + col
        place = (track // SHARD) * LANES + track % SHARD - n * 256
        near = hown[:, pl.ds(pl.multiple_of(n * 256, 256), 512)]
        total = jnp.dot(near, ones_at(place), preferred_element_type=jnp.float32)
        source = pos[:, cols]
        for m in range(BLOCKS // 2):
            total += jnp.dot(
                hpart[:, m * 512:(m + 1) * 512],
                ones_at(source - m * 512),
                preferred_element_type=jnp.float32,
            )

        @pl.when(n >= 2)
        def _():
            out_copy(n - 2, i).wait()

        stage[i] = (0.5 * total).astype(jnp.bfloat16)
        out_copy(n, i).start()

    for n in (tiles - 2, tiles - 1):
        out_copy(n, n % 2).wait()

    for i in range(CHUNKS):
        ex_copy(i).wait_send()
    for p in (0, 1):
        for k in range(4):
            if k:
                z_copy(p, k).wait_send()
            for d in (1, 2, 3):
                y_copy(p, k, d).wait_send()
                x_copy(p, k, d).wait_send()
            for dy in range(4):
                s_copy(p, k, dy).wait_send()


def fused(dw, rev, sep_in, head_in, sep_b, head_b, pos):
    dma = pltpu.SemaphoreType.DMA
    vmem = pl.BlockSpec(memory_space=pltpu.VMEM)
    return pl.pallas_call(
        kernel,
        out_shape=jax.ShapeDtypeStruct((ROWS, TRACKS), jnp.bfloat16),
        in_specs=[vmem] * 7,
        out_specs=pl.BlockSpec(memory_space=pl.ANY),
        scratch_shapes=[
            pltpu.VMEM((D, D), jnp.bfloat16),
            pltpu.VMEM((BLOCKS, D, 256), jnp.bfloat16),
            pltpu.VMEM((ROWS, D), jnp.bfloat16),
            pltpu.VMEM((ROWS, D), jnp.bfloat16),
            pltpu.VMEM((ROWS, BLOCKS * 256), jnp.bfloat16),
            pltpu.VMEM((ROWS, BLOCKS * 256), jnp.bfloat16),
            pltpu.VMEM((2, ROWS, 256), jnp.bfloat16),
            dma((2,)),
            dma((CHUNKS,)),
            dma((CHUNKS,)),
            dma((2, 3)),
            dma((2, 3)),
            dma((2, 4, 3)),
            dma((2, 4, 3)),
            dma((2, 4, 3)),
            dma((2, 4, 3)),
            dma((2, 4, 4)),
            dma((2, 4, 4)),
            dma((2,)),
        ],
        compiler_params=pltpu.CompilerParams(
            collective_id=0, has_side_effects=True, vmem_limit_bytes=60 * 1024 * 1024
        ),
    )(dw, rev, sep_in, head_in, sep_b, head_b, pos)


def per_device(
    coarse, skip, depth_kernel, sep_weight, sep_bias, head_weight, head_bias, strand_pair
):
    upsampled = jnp.repeat(coarse[0].astype(jnp.float32), 2, axis=0)
    merged = (upsampled + skip[0]).astype(jnp.bfloat16)
    padded = with_halo(merged, "seq", 1)
    depthwise = (
        depth_kernel[0] * padded[:-2]
        + depth_kernel[1] * padded[1:-1]
        + depth_kernel[2] * padded[2:]
    )
    depthwise = depthwise.astype(jnp.bfloat16)
    pos = (strand_pair // SHARD) * LANES + strand_pair % SHARD
    bias = jnp.pad(head_bias.reshape(-1, SHARD), ((0, 0), (0, LANES - SHARD)))
    preds = fused(
        depthwise,
        reversed_rows(depthwise),
        sep_weight,
        jnp.pad(head_weight, ((0, 0), (0, LANES - SHARD))),
        sep_bias[None],
        bias.reshape(1, -1),
        pos[None],
    )
    return preds[None]


def solution(mesh):
    in_specs = (
        P("batch", "seq", None),
        P("batch", "seq", None),
        P(),
        P("seq", None),
        P(),
        P(None, "seq"),
        P(),
        P(),
    )
    return jax.shard_map(
        per_device,
        mesh=mesh,
        in_specs=in_specs,
        out_specs=P("batch", "seq", None),
        check_vma=False,
    )
```

```python
import jax
import jax.numpy as jnp
from jax import lax
from jax.experimental import pallas as pl
from jax.experimental.pallas import tpu as pltpu
from jax.sharding import PartitionSpec as P

ROWS = 512
D = 1536
TRACKS = 3840
SHARD = 120
LANES = 128
BLOCKS = 16
SEP_ROWS = 48
QUARTER = 384
CHUNKS = 4
CHUNK = ROWS // CHUNKS
HALF = ROWS // 2
ALL = pl.ds(0, ROWS)
SHARED = (0,)
ORDER = (0, 1, 3, 2)


def gelu(v):
    return 0.5 * v * (1.0 + jnp.tanh(0.7978845608028654 * (v + 0.044715 * v * v * v)))


def softplus(v):
    return jnp.maximum(v, 0.0) + jnp.log1p(jnp.exp(-jnp.abs(v)))


def split(p, e, k):
    return p == 1 and (e == 2 or (e == 3 and k in SHARED))


def kernel(
    coarse, skip, depth, sep_in, head_in, sep_b, head_b, pos,
    out,
    wsep, whead, merged, dw, rev, mirrored, feat, featm, hown, hpart, perm, stage,
    local_sem, halo_send, halo_recv, ex_send, ex_recv, z_send, z_recv, y_send, y_recv,
    x_send, x_recv, s_send, s_recv, out_sem,
):
    s = lax.axis_index("seq")
    b = lax.axis_index("batch")
    c = s % 2
    y = (s // 2) % 4
    zl = s // 8
    x = b // 2
    zh = b % 2
    z = zh * 4 + zl
    u = (5 - zl) % 4
    ys = (y, y + 1 - 2 * (y % 2), (y + 2) % 4, 3 - y)

    def device(zz, yy, xx, cc):
        return {"seq": ((zz % 4) * 4 + yy) * 2 + cc, "batch": xx * 2 + zz // 4}

    mirror = {"seq": 31 - s, "batch": (b + 4) % 8}
    sibling = device(z, y, x, 1 - c)
    left = {"seq": (s + 31) % 32, "batch": b}
    right = {"seq": (s + 1) % 32, "batch": b}
    z_dev = [None] + [device((z + d) % 8, y, x, c) for d in (7, jnp.where(zl < 2, 6, 2), 1)]
    y_dev = [None] + [device(z, ys[e], x, c) for e in (1, 2, 3)]
    x_dev = [None] + [device(z, y, (x + d) % 4, c) for d in (1, 2, 3)]

    barrier = pltpu.get_barrier_semaphore()
    peers = [mirror, left, right] + z_dev[1:] + y_dev[1:] + x_dev[1:]
    for peer in peers:
        pl.semaphore_signal(barrier, inc=1, device_id=peer, device_id_type=pl.DeviceIdType.MESH)
    pl.semaphore_wait(barrier, len(peers))

    def slot(k, e):
        return ((zl + k) % 4) * 4 + ys[e]

    def view(p, j, cc, q=None):
        if p == 0:
            rows = pl.ds(pl.multiple_of((j * 2 + cc) * SEP_ROWS, 16), SEP_ROWS)
            if q is None:
                return wsep.at[rows, :]
            return wsep.at[rows, pl.ds(pl.multiple_of(q * QUARTER, LANES), QUARTER)]
        lanes = pl.ds(pl.multiple_of(cc * LANES, LANES), LANES)
        if q is None:
            return whead.at[j, :, lanes]
        return whead.at[j, pl.ds(pl.multiple_of(q * QUARTER, LANES), QUARTER), lanes]

    def own_view(p, q=None):
        if p == 0:
            if q is None:
                return sep_in
            return sep_in.at[:, pl.ds(pl.multiple_of(q * QUARTER, LANES), QUARTER)]
        if q is None:
            return head_in
        return head_in.at[pl.ds(pl.multiple_of(q * QUARTER, LANES), QUARTER), :]

    def copy(src, dst, send, recv, to):
        return pltpu.make_async_remote_copy(
            src_ref=src, dst_ref=dst, send_sem=send, recv_sem=recv,
            device_id=to, device_id_type=pl.DeviceIdType.MESH,
        )

    def z_copy(p, k):
        return copy(own_view(p), view(p, slot(0, 0), c), z_send.at[p, k - 1], z_recv.at[p, k - 1], z_dev[k])

    def y_copy(p, k, e):
        q = x if split(p, e, k) else None
        src = own_view(p, q) if k == 0 else view(p, slot(k, 0), c, q)
        return copy(src, view(p, slot(k, 0), c, q), y_send.at[p, k, e - 1], y_recv.at[p, k, e - 1], y_dev[e])

    def x_copy(p, k, e, d):
        ref = view(p, slot(k, e), c, x)
        return copy(ref, ref, x_send.at[p, e - 2, k, d - 1], x_recv.at[p, e - 2, k, d - 1], x_dev[d])

    def s_copy(p, k, e):
        src = own_view(p) if k == 0 and e == 0 else view(p, slot(k, e), c)
        return copy(src, view(p, slot(k, e), c), s_send.at[p, k, e], s_recv.at[p, k, e], sibling)

    def arrived(dst, recv):
        copy(dst, dst, s_send.at[0, 0, 0], recv, sibling).wait_recv()

    def z_wait(p, k):
        arrived(view(p, slot(k, 0), c), z_recv.at[p, k - 1])

    def y_wait(p, k, e):
        q = x if split(p, e, k) else None
        arrived(view(p, slot(k, e), c, q), y_recv.at[p, k, e - 1])

    def x_wait(p, k, e, d):
        arrived(view(p, slot(k, e), c, (x + 4 - d) % 4), x_recv.at[p, e - 2, k, d - 1])

    def s_wait(p, k, e):
        arrived(view(p, slot(k, e), 1 - c), s_recv.at[p, k, e])

    def ex_copy(i):
        rows = pl.ds(i * CHUNK, CHUNK)
        return copy(rev.at[rows, :], mirrored.at[rows, :], ex_send.at[i], ex_recv.at[i], mirror)

    middle = (zl == 1) | (zl == 2)

    def ex_some(near, chunks):
        @pl.when(middle if near else jnp.logical_not(middle))
        def _():
            for i in chunks:
                ex_copy(i).start()

    def spread(p, k, es=(2, 3, 1)):
        for e in es:
            y_copy(p, k, e).start()
        if 1 in es:
            s_copy(p, k, 0).start()

    def z_stage(p):
        for k in (1, 3, 2):
            z_wait(p, k)
            spread(p, k)

    def x_stage(p, e, items=ORDER):
        for k in items:
            if split(p, e, k):
                y_wait(p, k, e)
                for d in (2, 1, 3):
                    x_copy(p, k, e, d).start()

    def last_stage(p, e):
        for k in ORDER:
            if split(p, e, k):
                for d in (1, 3, 2):
                    x_wait(p, k, e, d)
            else:
                y_wait(p, k, e)
            s_copy(p, k, e).start()

    def from_sibling(p, e):
        for k in range(4):
            s_wait(p, k, e)

    def tile(n):
        return pl.ds(pl.multiple_of(n * 256, 256), 256)

    def features(block, dst):
        @pl.loop(0, D // 256)
        def _(n):
            v = jnp.dot(block[...], wsep[:, tile(n)], preferred_element_type=jnp.float32)
            dst[:, tile(n)] = gelu(v + sep_b[:, tile(n)]).astype(jnp.bfloat16)

    def head(block, dst, rows, e):
        @pl.loop(0, 4)
        def _(k):
            j = slot(k, e)
            v = jnp.dot(block[...], whead[j], preferred_element_type=jnp.float32)
            dst[rows, tile(j)] = softplus(v + head_b[:, tile(j)]).astype(jnp.bfloat16)

    locals_ = [
        pltpu.make_async_copy(own_view(p), view(p, slot(0, 0), c), local_sem.at[p]) for p in (0, 1)
    ]
    for cp in locals_:
        cp.start()
    for p in (0, 1):
        for k in (1, 3, 2):
            z_copy(p, k).start()
        spread(p, 0, (2, 3) if p else (2, 3, 1))

    i0 = lax.broadcasted_iota(jnp.int32, (ROWS, ROWS), 0)
    i1 = lax.broadcasted_iota(jnp.int32, (ROWS, ROWS), 1)
    up = jnp.where(i0[:, :ROWS // 2] // 2 == i1[:, :ROWS // 2], 1.0, 0.0).astype(jnp.bfloat16)

    @pl.loop(0, D // 256)
    def _(n):
        doubled = jnp.dot(up, coarse[:, tile(n)], preferred_element_type=jnp.float32)
        both = (doubled + skip[:, tile(n)].astype(jnp.float32)).astype(jnp.bfloat16)
        merged[8:8 + ROWS, tile(n)] = both.astype(jnp.float32)

    halos = [
        copy(merged.at[pl.ds(8, 8), :], merged.at[pl.ds(8 + ROWS, 8), :], halo_send.at[0], halo_recv.at[0], left),
        copy(merged.at[pl.ds(ROWS, 8), :], merged.at[pl.ds(0, 8), :], halo_send.at[1], halo_recv.at[1], right),
    ]
    for cp in halos:
        cp.start()
    flip = jnp.where(i0 + i1 == ROWS - 1, 1.0, 0.0).astype(jnp.bfloat16)
    for cp in halos:
        cp.wait_recv()

    @pl.when(s == 0)
    def _():
        merged[0:8, :] = jnp.zeros((8, D), jnp.float32)

    @pl.when(s == 31)
    def _():
        merged[8 + ROWS:16 + ROWS, :] = jnp.zeros((8, D), jnp.float32)

    @pl.loop(0, D // 256)
    def _(n):
        taps = depth[:, tile(n)]
        v = (
            taps[0:1] * merged[7:7 + ROWS, tile(n)]
            + taps[1:2] * merged[8:8 + ROWS, tile(n)]
            + taps[2:3] * merged[9:9 + ROWS, tile(n)]
        ).astype(jnp.bfloat16)
        dw[:, tile(n)] = v
        rev[:, tile(n)] = jnp.dot(flip, v, preferred_element_type=jnp.float32).astype(jnp.bfloat16)

    row = lax.broadcasted_iota(jnp.int32, (512, 256), 0)
    col = lax.broadcasted_iota(jnp.int32, (1, 256), 1)
    tiles = TRACKS // 256

    def ones_at(place, rows):
        return jnp.where(row[:rows] == place, 1.0, 0.0).astype(jnp.bfloat16)

    def moved(rows, n, es):
        source = pos[:, tile(n)]
        total = 0.0
        for e in es:
            for k in range(4):
                j = slot(k, e)
                total += jnp.dot(
                    hpart[rows, tile(j)],
                    ones_at(source - j * 256, 256),
                    preferred_element_type=jnp.float32,
                )
        return total

    def half_arrives(h):
        for i in range(h * CHUNKS // 2, (h + 1) * CHUNKS // 2):
            arrived(mirrored.at[pl.ds(i * CHUNK, CHUNK), :], ex_recv.at[i])
        rows = pl.ds(h * HALF, HALF)
        features(mirrored.at[rows, :], featm.at[rows, :])

    def partner(h, e):
        rows = pl.ds(h * HALF, HALF)
        head(featm.at[rows, :], hpart, rows, e)

    def early(h):
        rows = pl.ds(h * HALF, HALF)

        @pl.loop(0, tiles)
        def _(n):
            perm[rows, tile(n)] = moved(rows, n, (0, 1, 2)).astype(jnp.bfloat16)

    ex_some(True, (0, 1, 2, 3))
    z_stage(0)
    y_copy(1, 0, 1).start()
    s_copy(1, 0, 0).start()
    x_stage(0, 2)
    ex_some(False, (0, 1))
    z_stage(1)
    x_stage(1, 3)
    x_stage(1, 2, (0,))
    ex_some(False, (2,))
    for e in (1, 3, 2):
        last_stage(0, e)
    for cp in locals_:
        cp.wait()
    for e in (0, 1, 3, 2):
        from_sibling(0, e)
    x_stage(1, 2, (1,))
    ex_some(False, (3,))
    features(dw, feat)
    x_stage(1, 2, (3,))
    from_sibling(1, 0)
    head(feat, hown, ALL, 0)
    x_stage(1, 2, (2,))
    half_arrives(0)
    partner(0, 0)
    last_stage(1, 1)
    from_sibling(1, 1)
    head(feat, hown, ALL, 1)
    partner(0, 1)
    last_stage(1, 2)
    from_sibling(1, 2)
    head(feat, hown, ALL, 2)
    partner(0, 2)
    early(0)
    half_arrives(1)
    for e in (0, 1, 2):
        partner(1, e)
    last_stage(1, 3)
    early(1)
    from_sibling(1, 3)
    head(feat, hown, ALL, 3)
    head(featm, hpart, ALL, 3)

    def out_copy(n, i):
        return pltpu.make_async_copy(stage.at[i], out.at[:, tile(n)], out_sem.at[i])

    @pl.loop(0, tiles)
    def _(n):
        i = n % 2
        track = n * 256 + col
        place = (track // SHARD) * LANES + track % SHARD - n * 256
        near = hown[:, pl.ds(pl.multiple_of(n * 256, 256), 512)]
        total = jnp.dot(near, ones_at(place, 512), preferred_element_type=jnp.float32)
        total += moved(ALL, n, (3,))
        total += perm[:, tile(n)].astype(jnp.float32)

        @pl.when(n >= 2)
        def _():
            out_copy(n - 2, i).wait()

        stage[i] = (0.5 * total).astype(jnp.bfloat16)
        out_copy(n, i).start()

    for n in (tiles - 2, tiles - 1):
        out_copy(n, n % 2).wait()

    for cp in halos:
        cp.wait_send()
    for i in range(CHUNKS):
        ex_copy(i).wait_send()
    for p in (0, 1):
        for k in range(4):
            if k:
                z_copy(p, k).wait_send()
            for e in (1, 2, 3):
                y_copy(p, k, e).wait_send()
                if split(p, e, k):
                    for d in (1, 2, 3):
                        x_copy(p, k, e, d).wait_send()
            for e in range(4):
                s_copy(p, k, e).wait_send()


def fused(coarse, skip, depth, sep_in, head_in, sep_b, head_b, pos):
    dma = pltpu.SemaphoreType.DMA
    vmem = pl.BlockSpec(memory_space=pltpu.VMEM)
    return pl.pallas_call(
        kernel,
        out_shape=jax.ShapeDtypeStruct((ROWS, TRACKS), jnp.bfloat16),
        in_specs=[vmem] * 8,
        out_specs=pl.BlockSpec(memory_space=pl.ANY),
        scratch_shapes=[
            pltpu.VMEM((D, D), jnp.bfloat16),
            pltpu.VMEM((BLOCKS, D, 256), jnp.bfloat16),
            pltpu.VMEM((ROWS + 16, D), jnp.float32),
            pltpu.VMEM((ROWS, D), jnp.bfloat16),
            pltpu.VMEM((ROWS, D), jnp.bfloat16),
            pltpu.VMEM((ROWS, D), jnp.bfloat16),
            pltpu.VMEM((ROWS, D), jnp.bfloat16),
            pltpu.VMEM((ROWS, D), jnp.bfloat16),
            pltpu.VMEM((ROWS, BLOCKS * 256), jnp.bfloat16),
            pltpu.VMEM((ROWS, BLOCKS * 256), jnp.bfloat16),
            pltpu.VMEM((ROWS, TRACKS), jnp.bfloat16),
            pltpu.VMEM((2, ROWS, 256), jnp.bfloat16),
            dma((2,)),
            dma((2,)),
            dma((2,)),
            dma((CHUNKS,)),
            dma((CHUNKS,)),
            dma((2, 3)),
            dma((2, 3)),
            dma((2, 4, 3)),
            dma((2, 4, 3)),
            dma((2, 2, 4, 3)),
            dma((2, 2, 4, 3)),
            dma((2, 4, 4)),
            dma((2, 4, 4)),
            dma((2,)),
        ],
        compiler_params=pltpu.CompilerParams(
            collective_id=0, has_side_effects=True, vmem_limit_bytes=60 * 1024 * 1024
        ),
    )(coarse, skip, depth, sep_in, head_in, sep_b, head_b, pos)


def per_device(
    coarse, skip, depth_kernel, sep_weight, sep_bias, head_weight, head_bias, strand_pair
):
    pos = (strand_pair // SHARD) * LANES + strand_pair % SHARD
    bias = jnp.pad(head_bias.reshape(-1, SHARD), ((0, 0), (0, LANES - SHARD)))
    preds = fused(
        coarse[0],
        skip[0],
        depth_kernel,
        sep_weight,
        jnp.pad(head_weight, ((0, 0), (0, LANES - SHARD))),
        sep_bias[None],
        bias.reshape(1, -1),
        pos[None],
    )
    return preds[None]


def solution(mesh):
    in_specs = (
        P("batch", "seq", None),
        P("batch", "seq", None),
        P(),
        P("seq", None),
        P(),
        P(None, "seq"),
        P(),
        P(),
    )
    return jax.shard_map(
        per_device,
        mesh=mesh,
        in_specs=in_specs,
        out_specs=P("batch", "seq", None),
        check_vma=False,
    )
```

```python
import jax
import jax.numpy as jnp
from jax import lax
from jax.experimental import pallas as pl
from jax.experimental.pallas import tpu as pltpu
from jax.sharding import PartitionSpec as P

ROWS = 512
D = 1536
TRACKS = 3840
SHARD = 120
LANES = 128
BLOCKS = 16
SEP_ROWS = 48
QUARTER = 384
CHUNKS = 4
CHUNK = ROWS // CHUNKS
HALF = ROWS // 2
ALL = pl.ds(0, ROWS)
SHARED = (0,)
ORDER = (0, 1, 3, 2)


def gelu(v):
    return 0.5 * v * (1.0 + jnp.tanh(0.7978845608028654 * (v + 0.044715 * v * v * v)))


def softplus(v):
    return jnp.maximum(v, 0.0) + jnp.log1p(jnp.exp(-jnp.abs(v)))


def split(p, e, k):
    return p == 1 and (e == 2 or (e == 3 and k in SHARED))


def kernel(
    coarse, skip, depth, sep_in, head_in, vectors,
    out,
    wsep, whead, merged, dw, rev, mirrored, feat, featm, hown, hpart, perm, stage,
    local_sem, halo_send, halo_recv, ex_send, ex_recv, z_send, z_recv, y_send, y_recv,
    x_send, x_recv, s_send, s_recv, out_sem,
):
    s = lax.axis_index("seq")
    b = lax.axis_index("batch")
    c = s % 2
    y = (s // 2) % 4
    zl = s // 8
    x = b // 2
    zh = b % 2
    z = zh * 4 + zl
    u = (5 - zl) % 4
    ys = (y, y + 1 - 2 * (y % 2), (y + 2) % 4, 3 - y)

    def device(zz, yy, xx, cc):
        return {"seq": ((zz % 4) * 4 + yy) * 2 + cc, "batch": xx * 2 + zz // 4}

    mirror = {"seq": 31 - s, "batch": (b + 4) % 8}
    sibling = device(z, y, x, 1 - c)
    left = {"seq": (s + 31) % 32, "batch": b}
    right = {"seq": (s + 1) % 32, "batch": b}
    z_dev = [None] + [device((z + d) % 8, y, x, c) for d in (7, jnp.where(zl < 2, 6, 2), 1)]
    y_dev = [None] + [device(z, ys[e], x, c) for e in (1, 2, 3)]
    x_dev = [None] + [device(z, y, (x + d) % 4, c) for d in (1, 2, 3)]

    barrier = pltpu.get_barrier_semaphore()
    peers = [mirror, left, right] + z_dev[1:] + y_dev[1:] + x_dev[1:]
    for peer in peers:
        pl.semaphore_signal(barrier, inc=1, device_id=peer, device_id_type=pl.DeviceIdType.MESH)
    pl.semaphore_wait(barrier, len(peers))

    def slot(k, e):
        return ((zl + k) % 4) * 4 + ys[e]

    def view(p, j, cc, q=None):
        if p == 0:
            rows = pl.ds(pl.multiple_of((j * 2 + cc) * SEP_ROWS, 16), SEP_ROWS)
            if q is None:
                return wsep.at[rows, :]
            return wsep.at[rows, pl.ds(pl.multiple_of(q * QUARTER, LANES), QUARTER)]
        lanes = pl.ds(pl.multiple_of(cc * LANES, LANES), LANES)
        if q is None:
            return whead.at[j, :, lanes]
        return whead.at[j, pl.ds(pl.multiple_of(q * QUARTER, LANES), QUARTER), lanes]

    def own_view(p, q=None):
        if p == 0:
            if q is None:
                return sep_in
            return sep_in.at[:, pl.ds(pl.multiple_of(q * QUARTER, LANES), QUARTER)]
        if q is None:
            return head_in
        return head_in.at[pl.ds(pl.multiple_of(q * QUARTER, LANES), QUARTER), :]

    def copy(src, dst, send, recv, to):
        return pltpu.make_async_remote_copy(
            src_ref=src, dst_ref=dst, send_sem=send, recv_sem=recv,
            device_id=to, device_id_type=pl.DeviceIdType.MESH,
        )

    def z_copy(p, k):
        return copy(own_view(p), view(p, slot(0, 0), c), z_send.at[p, k - 1], z_recv.at[p, k - 1], z_dev[k])

    def y_copy(p, k, e):
        q = x if split(p, e, k) else None
        src = own_view(p, q) if k == 0 else view(p, slot(k, 0), c, q)
        return copy(src, view(p, slot(k, 0), c, q), y_send.at[p, k, e - 1], y_recv.at[p, k, e - 1], y_dev[e])

    def x_copy(p, k, e, d):
        ref = view(p, slot(k, e), c, x)
        return copy(ref, ref, x_send.at[p, e - 2, k, d - 1], x_recv.at[p, e - 2, k, d - 1], x_dev[d])

    def s_copy(p, k, e):
        src = own_view(p) if k == 0 and e == 0 else view(p, slot(k, e), c)
        return copy(src, view(p, slot(k, e), c), s_send.at[p, k, e], s_recv.at[p, k, e], sibling)

    def arrived(dst, recv):
        copy(dst, dst, s_send.at[0, 0, 0], recv, sibling).wait_recv()

    def z_wait(p, k):
        arrived(view(p, slot(k, 0), c), z_recv.at[p, k - 1])

    def y_wait(p, k, e):
        q = x if split(p, e, k) else None
        arrived(view(p, slot(k, e), c, q), y_recv.at[p, k, e - 1])

    def x_wait(p, k, e, d):
        arrived(view(p, slot(k, e), c, (x + 4 - d) % 4), x_recv.at[p, e - 2, k, d - 1])

    def s_wait(p, k, e):
        arrived(view(p, slot(k, e), 1 - c), s_recv.at[p, k, e])

    def ex_copy(i):
        rows = pl.ds(i * CHUNK, CHUNK)
        return copy(rev.at[rows, :], mirrored.at[rows, :], ex_send.at[i], ex_recv.at[i], mirror)

    middle = (zl == 1) | (zl == 2)

    def ex_some(near, chunks):
        @pl.when(middle if near else jnp.logical_not(middle))
        def _():
            for i in chunks:
                ex_copy(i).start()

    def spread(p, k, es=(2, 3, 1)):
        for e in es:
            y_copy(p, k, e).start()
        if 1 in es:
            s_copy(p, k, 0).start()

    def z_stage(p):
        for k in (1, 3, 2):
            z_wait(p, k)
            spread(p, k)

    def x_stage(p, e, items=ORDER):
        for k in items:
            if split(p, e, k):
                y_wait(p, k, e)
                for d in (2, 1, 3):
                    x_copy(p, k, e, d).start()

    def last_stage(p, e):
        for k in ORDER:
            if split(p, e, k):
                for d in (1, 3, 2):
                    x_wait(p, k, e, d)
            else:
                y_wait(p, k, e)
            s_copy(p, k, e).start()

    def from_sibling(p, e):
        for k in range(4):
            s_wait(p, k, e)

    def tile(n):
        return pl.ds(pl.multiple_of(n * 256, 256), 256)

    def features(block, dst):
        @pl.loop(0, D // 256)
        def _(n):
            v = jnp.dot(block[...], wsep[:, tile(n)], preferred_element_type=jnp.float32)
            dst[:, tile(n)] = gelu(v + vectors[:, tile(n)]).astype(jnp.bfloat16)

    def head(block, dst, rows, e):
        @pl.loop(0, 4)
        def _(k):
            j = slot(k, e)
            v = jnp.dot(block[...], whead[j], preferred_element_type=jnp.float32)
            dst[rows, tile(j)] = softplus(v + vectors[:, tile(D // 256 + j)]).astype(jnp.bfloat16)

    locals_ = [
        pltpu.make_async_copy(own_view(p), view(p, slot(0, 0), c), local_sem.at[p]) for p in (0, 1)
    ]
    for cp in locals_:
        cp.start()
    for p in (0, 1):
        for k in (1, 3, 2):
            z_copy(p, k).start()
        spread(p, 0, (2, 3) if p else (2, 3, 1))

    i0 = lax.broadcasted_iota(jnp.int32, (ROWS, ROWS), 0)
    i1 = lax.broadcasted_iota(jnp.int32, (ROWS, ROWS), 1)
    up = jnp.where(i0[:, :ROWS // 2] // 2 == i1[:, :ROWS // 2], 1.0, 0.0).astype(jnp.bfloat16)

    @pl.loop(0, D // 256)
    def _(n):
        doubled = jnp.dot(up, coarse[:, tile(n)], preferred_element_type=jnp.float32)
        both = (doubled + skip[:, tile(n)].astype(jnp.float32)).astype(jnp.bfloat16)
        merged[8:8 + ROWS, tile(n)] = both.astype(jnp.float32)

    halos = [
        copy(merged.at[pl.ds(8, 8), :], merged.at[pl.ds(8 + ROWS, 8), :], halo_send.at[0], halo_recv.at[0], left),
        copy(merged.at[pl.ds(ROWS, 8), :], merged.at[pl.ds(0, 8), :], halo_send.at[1], halo_recv.at[1], right),
    ]
    for cp in halos:
        cp.start()
    flip = jnp.where(i0 + i1 == ROWS - 1, 1.0, 0.0).astype(jnp.bfloat16)
    for cp in halos:
        cp.wait_recv()

    @pl.when(s == 0)
    def _():
        merged[0:8, :] = jnp.zeros((8, D), jnp.float32)

    @pl.when(s == 31)
    def _():
        merged[8 + ROWS:16 + ROWS, :] = jnp.zeros((8, D), jnp.float32)

    @pl.loop(0, D // 256)
    def _(n):
        taps = depth[:, tile(n)]
        v = (
            taps[0:1] * merged[7:7 + ROWS, tile(n)]
            + taps[1:2] * merged[8:8 + ROWS, tile(n)]
            + taps[2:3] * merged[9:9 + ROWS, tile(n)]
        ).astype(jnp.bfloat16)
        dw[:, tile(n)] = v
        rev[:, tile(n)] = jnp.dot(flip, v, preferred_element_type=jnp.float32).astype(jnp.bfloat16)

    row = lax.broadcasted_iota(jnp.int32, (512, 256), 0)
    col = lax.broadcasted_iota(jnp.int32, (1, 256), 1)
    tiles = TRACKS // 256

    def ones_at(place, rows):
        return jnp.where(row[:rows] == place, 1.0, 0.0).astype(jnp.bfloat16)

    def moved(rows, n, es):
        source = vectors[:, tile(D // 256 + BLOCKS + n)].astype(jnp.int32)
        total = 0.0
        for e in es:
            for k in range(4):
                j = slot(k, e)
                total += jnp.dot(
                    hpart[rows, tile(j)],
                    ones_at(source - j * 256, 256),
                    preferred_element_type=jnp.float32,
                )
        return total

    def half_arrives(h):
        for i in range(h * CHUNKS // 2, (h + 1) * CHUNKS // 2):
            arrived(mirrored.at[pl.ds(i * CHUNK, CHUNK), :], ex_recv.at[i])
        rows = pl.ds(h * HALF, HALF)
        features(mirrored.at[rows, :], featm.at[rows, :])

    def partner(h, e):
        rows = pl.ds(h * HALF, HALF)
        head(featm.at[rows, :], hpart, rows, e)

    def early(h):
        rows = pl.ds(h * HALF, HALF)

        @pl.loop(0, tiles)
        def _(n):
            perm[rows, tile(n)] = moved(rows, n, (0, 1, 2)).astype(jnp.bfloat16)

    ex_some(True, (0, 1, 2, 3))
    z_stage(0)
    y_copy(1, 0, 1).start()
    s_copy(1, 0, 0).start()
    x_stage(0, 2)
    ex_some(False, (0, 1))
    z_stage(1)
    x_stage(1, 3)
    x_stage(1, 2, (0,))
    ex_some(False, (2,))
    for e in (1, 3, 2):
        last_stage(0, e)
    for cp in locals_:
        cp.wait()
    for e in (0, 1, 3, 2):
        from_sibling(0, e)
    x_stage(1, 2, (1,))
    ex_some(False, (3,))
    features(dw, feat)
    x_stage(1, 2, (3,))
    from_sibling(1, 0)
    head(feat, hown, ALL, 0)
    x_stage(1, 2, (2,))
    half_arrives(0)
    partner(0, 0)
    last_stage(1, 1)
    from_sibling(1, 1)
    head(feat, hown, ALL, 1)
    partner(0, 1)
    last_stage(1, 2)
    from_sibling(1, 2)
    head(feat, hown, ALL, 2)
    partner(0, 2)
    early(0)
    half_arrives(1)
    for e in (0, 1, 2):
        partner(1, e)
    last_stage(1, 3)
    early(1)
    from_sibling(1, 3)
    head(feat, hown, ALL, 3)
    head(featm, hpart, ALL, 3)

    def out_copy(n, i):
        return pltpu.make_async_copy(stage.at[i], out.at[:, tile(n)], out_sem.at[i])

    @pl.loop(0, tiles)
    def _(n):
        i = n % 2
        track = n * 256 + col
        place = (track // SHARD) * LANES + track % SHARD - n * 256
        near = hown[:, pl.ds(pl.multiple_of(n * 256, 256), 512)]
        total = jnp.dot(near, ones_at(place, 512), preferred_element_type=jnp.float32)
        total += moved(ALL, n, (3,))
        total += perm[:, tile(n)].astype(jnp.float32)

        @pl.when(n >= 2)
        def _():
            out_copy(n - 2, i).wait()

        stage[i] = (0.5 * total).astype(jnp.bfloat16)
        out_copy(n, i).start()

    for n in (tiles - 2, tiles - 1):
        out_copy(n, n % 2).wait()

    for cp in halos:
        cp.wait_send()
    for i in range(CHUNKS):
        ex_copy(i).wait_send()
    for p in (0, 1):
        for k in range(4):
            if k:
                z_copy(p, k).wait_send()
            for e in (1, 2, 3):
                y_copy(p, k, e).wait_send()
                if split(p, e, k):
                    for d in (1, 2, 3):
                        x_copy(p, k, e, d).wait_send()
            for e in range(4):
                s_copy(p, k, e).wait_send()


def fused(coarse, skip, depth, sep_in, head_in, vectors):
    dma = pltpu.SemaphoreType.DMA
    vmem = pl.BlockSpec(memory_space=pltpu.VMEM)
    return pl.pallas_call(
        kernel,
        out_shape=jax.ShapeDtypeStruct((ROWS, TRACKS), jnp.bfloat16),
        in_specs=[vmem] * 6,
        out_specs=pl.BlockSpec(memory_space=pl.ANY),
        scratch_shapes=[
            pltpu.VMEM((D, D), jnp.bfloat16),
            pltpu.VMEM((BLOCKS, D, 256), jnp.bfloat16),
            pltpu.VMEM((ROWS + 16, D), jnp.float32),
            pltpu.VMEM((ROWS, D), jnp.bfloat16),
            pltpu.VMEM((ROWS, D), jnp.bfloat16),
            pltpu.VMEM((ROWS, D), jnp.bfloat16),
            pltpu.VMEM((ROWS, D), jnp.bfloat16),
            pltpu.VMEM((ROWS, D), jnp.bfloat16),
            pltpu.VMEM((ROWS, BLOCKS * 256), jnp.bfloat16),
            pltpu.VMEM((ROWS, BLOCKS * 256), jnp.bfloat16),
            pltpu.VMEM((ROWS, TRACKS), jnp.bfloat16),
            pltpu.VMEM((2, ROWS, 256), jnp.bfloat16),
            dma((2,)),
            dma((2,)),
            dma((2,)),
            dma((CHUNKS,)),
            dma((CHUNKS,)),
            dma((2, 3)),
            dma((2, 3)),
            dma((2, 4, 3)),
            dma((2, 4, 3)),
            dma((2, 2, 4, 3)),
            dma((2, 2, 4, 3)),
            dma((2, 4, 4)),
            dma((2, 4, 4)),
            dma((2,)),
        ],
        compiler_params=pltpu.CompilerParams(
            collective_id=0, has_side_effects=True, vmem_limit_bytes=60 * 1024 * 1024
        ),
    )(coarse, skip, depth, sep_in, head_in, vectors)


def per_device(
    coarse, skip, depth_kernel, sep_weight, sep_bias, head_weight, head_bias, strand_pair
):
    pos = (strand_pair // SHARD) * LANES + strand_pair % SHARD
    bias = jnp.pad(head_bias.reshape(-1, SHARD), ((0, 0), (0, LANES - SHARD)))
    vectors = jnp.concatenate([sep_bias, bias.reshape(-1), pos.astype(jnp.float32)])
    preds = fused(
        coarse[0],
        skip[0],
        depth_kernel,
        sep_weight,
        jnp.pad(head_weight, ((0, 0), (0, LANES - SHARD))),
        vectors[None],
    )
    return preds[None]


def solution(mesh):
    in_specs = (
        P("batch", "seq", None),
        P("batch", "seq", None),
        P(),
        P("seq", None),
        P(),
        P(None, "seq"),
        P(),
        P(),
    )
    return jax.shard_map(
        per_device,
        mesh=mesh,
        in_specs=in_specs,
        out_specs=P("batch", "seq", None),
        check_vma=False,
    )
```
